32 devices in a mesh: row: 8 (over z, x), col: 4 (over y, core).
Axes of the slice: x: 2, y: 2, z: 4, core: 2. Of those that a mesh axis runs over, the one named last changes fastest.
Arguments:
- x_act: bfloat16 [512, 3072], P('col', 'row'), may hold values from -0.1875 to 0.1875
- grad_pre: bfloat16 [512, 8192], P('row', 'col'), may hold values from -6 to 6
- weight_blocks: bfloat16 [8, 4, 12, 128, 128], P('row', 'col'), may hold values from -0.1875 to 0.1875
- block_coord: int32 [8, 4, 12], P('row', 'col'), may hold values from -1 to 47, as said below
Outputs:
- grad_input: bfloat16 [512, 3072], P('col', 'row')
- grad_weight: bfloat16 [8, 4, 12, 128, 128], P('row', 'col')
The draws below stay inside these ranges and needn't reach their ends.
Inputs may be any that keep to these rules, and one draw needn't show every extreme that they name: `block_coord`: in each tile the live slots come first and hold distinct local block numbers r * 16 + c (block row r, block column c of the tile) in ascending order; the remaining slots hold -1. Each tile has 1 to 12 live slots and some tile has all 12 live; values in the empty slots of weight_blocks are not read.
All inputs are finite; a program needn't handle non-finite values.
Results may differ from the reference program's by a relative error of at most 0.001.
Values may be sent and summed in bfloat16 or wider, within the bound.
A program may use at most 64 MiB of HBM per device.

```python
import jax
import jax.numpy as jnp
from jax import lax

BLK = 128
BLK_R = 3
BLK_C = 16
CAP = 12
D = 3072
FF = 8192
TOKENS = 512
N_ROW = 8
N_COL = 4


def draw_block_coord(key, part):
    tile_count = N_ROW * N_COL
    spot_count = BLK_R * BLK_C
    key_count, key_full, key_pick, key_order = jax.random.split(key, 4)
    counts = jax.random.randint(key_count, (tile_count,), 1, CAP * 3 // 4 + 1)
    filled = jax.random.randint(key_full, (tile_count,), 0, 8) == 0
    chosen = jnp.arange(tile_count) == jax.random.randint(key_pick, (), 0, tile_count)
    counts = jnp.where(filled | chosen, CAP, counts)
    tile_keys = jax.random.split(key_order, tile_count)
    shuffled = jax.vmap(lambda one_key: jax.random.permutation(one_key, spot_count))(tile_keys)[:, :CAP]
    slot_index = jnp.arange(CAP)[None, :]
    picked = jnp.where(slot_index < counts[:, None], shuffled, spot_count)
    picked = jnp.sort(picked, axis=1)
    picked = jnp.where(picked == spot_count, -1, picked)
    return picked.reshape(N_ROW, N_COL, CAP).astype(jnp.int32)


def levels(key, shape, cuts, least, largest):
    level = 1.0
    for dim, shards_of in cuts:
        heights = jax.random.uniform(jax.random.fold_in(jax.random.fold_in(key, 6), dim), (shards_of,), jnp.float32, least / len(cuts), largest / len(cuts))
        level = level * jnp.repeat(jnp.exp(heights), shape[dim] // shards_of).reshape((-1,) + (1,) * (len(shape) - 1 - dim))
    return level


def noise(stream_key, shape, scale, bound, cuts=(), kind=jnp.bfloat16):
    gain = levels(stream_key, shape, cuts, -0.22, 0.18) if cuts else 1.0
    values = jax.random.normal(stream_key, shape, jnp.float32) * scale * gain
    return jnp.minimum(jnp.maximum(values, -bound), bound).astype(kind)


def setup_inputs(seed: int = 0) -> dict:
    splits = jax.random.split(jax.random.key(seed), 5)
    x_act = noise(splits[0], (TOKENS, D), 0.03, 0.1875, ((0, 4), (1, 8)))
    grad_pre = noise(splits[1], (TOKENS, FF), 1.0, 6.0, ((0, 8), (1, 4)))
    weight_blocks = noise(splits[2], (N_ROW, N_COL, CAP, BLK, BLK), (BLK * CAP * N_COL // (2 * BLK_R)) ** -0.5, 0.1875, ((0, 8), (1, 4)))
    block_coord = draw_block_coord(jax.random.fold_in(splits[4], 71), 0)
    return {"x_act": x_act, "grad_pre": grad_pre, "weight_blocks": weight_blocks, "block_coord": block_coord}


def tile_grads(x_panel, grad_panel, weights, coord):
    live_slot = coord >= 0
    safe_coord = jnp.where(live_slot, coord, 0)
    block_row = (safe_coord // BLK_C).astype(jnp.int32)
    block_col = (safe_coord % BLK_C).astype(jnp.int32)
    row_hot = ((block_row[:, None] == jnp.arange(BLK_R, dtype=jnp.int32)[None, :]) & live_slot[:, None]).astype(jnp.float32)
    x_slots = jnp.take(x_panel, block_row, axis=1)
    grad_slots = jnp.take(grad_panel, block_col, axis=1)
    w_term = jnp.einsum('tsa,tsb->sab', x_slots, grad_slots, precision=lax.Precision.HIGHEST)
    w_term = jnp.where(live_slot[:, None, None], w_term, jnp.float32(0.0))
    spread = jnp.einsum('tsb,sab->tsa', grad_slots, weights.astype(jnp.float32), precision=lax.Precision.HIGHEST)
    x_term = jnp.einsum('tsa,sr->tra', spread, row_hot, precision=lax.Precision.HIGHEST)
    return w_term, x_term


def reference(x_act, grad_pre, weight_blocks, block_coord):
    x_grid = x_act.astype(jnp.float32).reshape(TOKENS, N_ROW, BLK_R, BLK)
    grad_grid = grad_pre.astype(jnp.float32).reshape(TOKENS, N_COL, BLK_C, BLK)

    def one_row(row_index):
        x_panel = lax.dynamic_index_in_dim(x_grid, row_index, 1, keepdims=False)

        def one_col(running, col_index):
            grad_panel = lax.dynamic_index_in_dim(grad_grid, col_index, 1, keepdims=False)
            w_term, x_term = tile_grads(x_panel, grad_panel, weight_blocks[row_index, col_index], block_coord[row_index, col_index])
            return running + x_term, w_term.astype(jnp.bfloat16)

        start_sum = jnp.zeros((TOKENS, BLK_R, BLK), jnp.float32)
        running, w_rows = lax.scan(one_col, start_sum, jnp.arange(N_COL, dtype=jnp.int32))
        return running.astype(jnp.bfloat16), w_rows

    x_rows, grad_weight = lax.map(one_row, jnp.arange(N_ROW, dtype=jnp.int32))
    grad_input = jnp.transpose(x_rows, (1, 0, 2, 3)).reshape(TOKENS, N_ROW * BLK_R * BLK)
    return grad_input, grad_weight
```

```python
import functools

import jax
import jax.numpy as jnp
from jax import lax
from jax.experimental import pallas as pl
from jax.experimental.pallas import tpu as pltpu
from jax.sharding import PartitionSpec as P

MESH = pl.DeviceIdType.MESH
CORES = 2
CHUNKS = 2
F32 = jnp.float32
BF16 = jnp.bfloat16


def either(a, b):
    if a is True or b is True:
        return True
    if a is False:
        return b
    if b is False:
        return a
    return jnp.logical_or(a, b)


def both(a, b):
    if a is False or b is False:
        return False
    if a is True:
        return b
    if b is True:
        return a
    return jnp.logical_and(a, b)


def negate(a):
    return (not a) if isinstance(a, bool) else jnp.logical_not(a)


def when(cond, body):
    if cond is True:
        body()
    elif cond is not False:
        pl.when(cond)(body)


def kernel(
    rows, cols, coord_ref, x_ref, g_ref, w_ref, gi_ref, gw_ref,
    g_all, x_all, x_t, w_own, w_t, dense, part, pair_in, y_in,
    local_sem, g_send, g_recv, x_send, x_recv, pair_send, pair_recv, y_send, y_recv,
):
    hi_n = 4 if rows % 4 == 0 else 1
    lo_n = rows // hi_n
    y_n = cols // CORES
    slots, blk = w_own.shape[0], w_own.shape[1]
    tokens = g_all.shape[1]
    step_rows = tokens // CHUNKS
    row_blocks = x_t.shape[0] // blk
    col_blocks = g_all.shape[2] // blk
    per_group = rows // cols

    row = lax.axis_index("row")
    col = lax.axis_index("col")
    hi, lo = lax.div(row, lo_n), lax.rem(row, lo_n)
    y, core = lax.div(col, CORES), lax.rem(col, CORES)
    sibling = (row, y * CORES + (1 - core))
    own = row

    def peer_y(dist):
        return lax.rem(y + dist, y_n)

    directions = (
        (hi < hi_n - 1, (row + lo_n, col)),
        (hi > 0, (row - lo_n, col)),
        (lo < lo_n - 1, (row + 1, col)),
        (lo > 0, (row - 1, col)),
    )

    own_g = pltpu.make_async_copy(g_ref, g_all.at[own], local_sem.at[0])
    own_x = pltpu.make_async_copy(x_ref, x_all.at[col], local_sem.at[1])
    own_w = pltpu.make_async_copy(w_ref, w_own, local_sem.at[2])
    own_w.start()
    own_g.start()
    own_x.start()

    barrier = pltpu.get_barrier_semaphore()
    count = jnp.int32(y_n)
    for there, device in directions:
        count = count + there.astype(jnp.int32)

        def greet(device=device):
            pl.semaphore_signal(barrier, inc=1, device_id=device, device_id_type=MESH)

        when(there, greet)
    pl.semaphore_signal(barrier, inc=1, device_id=sibling, device_id_type=MESH)
    for dist in range(1, y_n):
        pl.semaphore_signal(
            barrier, inc=1, device_id=(row, peer_y(dist) * CORES + core), device_id_type=MESH
        )
    pl.semaphore_wait(barrier, count)

    def g_copy(block, chunk, direction, from_input=False):
        span = pl.ds(chunk * step_rows, step_rows)
        there = g_all.at[block, span]
        return pltpu.make_async_remote_copy(
            src_ref=g_ref.at[span] if from_input else there,
            dst_ref=there,
            send_sem=g_send.at[direction, block, chunk],
            recv_sem=g_recv.at[block, chunk],
            device_id=directions[direction][1],
            device_id_type=MESH,
        )

    def sends(dh, dl, chunk):
        origin = hi + dh
        swapped = False
        if chunk == CHUNKS - 1:
            swapped = jnp.logical_or(origin == 0, origin == hi_n - 1)
        along_hi = either(swapped, dl == 0)
        along_lo = either(negate(swapped), dh == 0)
        conds = (
            both(along_hi, dh <= 0), both(along_hi, dh >= 0),
            both(along_lo, dl <= 0), both(along_lo, dl >= 0),
        )
        return [both(cond, directions[n][0]) for n, cond in enumerate(conds)]

    def valid(dh, dl):
        cond = True
        if dh > 0:
            cond = both(cond, hi + dh < hi_n)
        if dh < 0:
            cond = both(cond, hi + dh >= 0)
        if dl > 0:
            cond = both(cond, lo + dl < lo_n)
        if dl < 0:
            cond = both(cond, lo + dl >= 0)
        return cond

    def block_of(dh, dl):
        return row + (dh * lo_n + dl)

    def forward(dh, dl, chunk):
        for n, cond in enumerate(sends(dh, dl, chunk)):
            when(cond, lambda n=n: g_copy(block_of(dh, dl), chunk, n, dh == 0 and dl == 0).start())

    def arrive(dh, dl, chunk):
        def body():
            g_copy(block_of(dh, dl), chunk, 0).wait_recv()
            forward(dh, dl, chunk)

        when(valid(dh, dl), body)

    def drain(dh, dl, chunk):
        def body():
            for n, cond in enumerate(sends(dh, dl, chunk)):
                when(cond, lambda n=n: g_copy(block_of(dh, dl), chunk, n, dh == 0 and dl == 0).wait_send())

        when(valid(dh, dl), body)

    def x_copy(index, group, device, from_input=False):
        return pltpu.make_async_remote_copy(
            src_ref=x_ref if from_input else x_all.at[group],
            dst_ref=x_all.at[group],
            send_sem=x_send.at[index],
            recv_sem=x_recv.at[group],
            device_id=device,
            device_id_type=MESH,
        )

    def x_to_y(dist):
        return x_copy(dist, col, (row, peer_y(dist) * CORES + core), True)

    def x_to_sibling(dist):
        return x_copy(y_n + dist, peer_y(dist) * CORES + core, sibling, dist == 0)

    def x_from_sibling(dist):
        return x_copy(0, peer_y(dist) * CORES + (1 - core), sibling)

    def group_of(block):
        return lax.div(block, per_group)

    def mine(block):
        return lax.rem(group_of(block), CORES) == core

    def pair_copy(block):
        return pltpu.make_async_remote_copy(
            src_ref=part.at[block],
            dst_ref=pair_in.at[block],
            send_sem=pair_send.at[block],
            recv_sem=pair_recv.at[block],
            device_id=sibling,
            device_id_type=MESH,
        )

    def y_copy(block):
        sub = lax.rem(block, per_group)
        return pltpu.make_async_remote_copy(
            src_ref=part.at[block],
            dst_ref=y_in.at[y, sub],
            send_sem=y_send.at[block],
            recv_sem=y_recv.at[y, sub],
            device_id=(row, group_of(block)),
            device_id_type=MESH,
        )

    def compute(dh, dl):
        def body():
            block = block_of(dh, dl)
            part[block] = jnp.dot(g_all[block], dense[...], preferred_element_type=F32)
            when(negate(mine(block)), lambda: pair_copy(block).start())

        when(valid(dh, dl), body)

    def finish(dh, dl):
        def body():
            block = block_of(dh, dl)

            def reduce():
                pair_copy(block).wait_recv()
                part[block] = part[block] + pair_in[block]
                when(group_of(block) != col, lambda: y_copy(block).start())

            when(mine(block), reduce)

        when(valid(dh, dl), body)

    for chunk in range(CHUNKS):
        forward(0, 0, chunk)
    for dist in range(1, y_n):
        x_to_y(dist).start()
    x_to_sibling(0).start()

    own_w.wait()

    def turn(s, carry):
        w_t[s] = w_own[s].T
        return carry

    lax.fori_loop(0, slots, turn, 0)

    def spread(c, carry):
        for r in range(row_blocks):
            total = jnp.zeros((blk, blk), BF16)
            for s in range(slots):
                hit = (coord_ref[0, s] == r * col_blocks + c).astype(F32)
                total = total + w_t[s] * jnp.full((blk, blk), hit, F32).astype(BF16)
            dense[pl.ds(pl.multiple_of(c * blk, blk), blk), r * blk:(r + 1) * blk] = total
        return carry

    lax.fori_loop(0, col_blocks, spread, 0)

    own_g.wait()
    own_x.wait()
    compute(0, 0)

    steps = []
    for t in range(1, hi_n + lo_n - 1):
        step = []
        for far in range(min(t, hi_n - 1), -1, -1):
            side = t - far
            if side >= lo_n:
                continue
            for dh in sorted({far, -far}):
                for dl in sorted({side, -side}):
                    step.append((dh, dl))
        steps.append(step)

    pending = [(0, 0)]
    for index, step in enumerate(steps):
        for chunk in range(CHUNKS):
            for dh, dl in step:
                arrive(dh, dl, chunk)
        if index == 0:
            for dist in range(1, y_n):
                x_copy(0, peer_y(dist) * CORES + core, sibling).wait_recv()
                x_to_sibling(dist).start()
        for dh, dl in step:
            compute(dh, dl)
        if index < len(steps) - 1:
            for dh, dl in pending:
                finish(dh, dl)
            pending = []
        pending = pending + step
        if index == min(1, len(steps) - 1):
            for dist in range(y_n):
                x_from_sibling(dist).wait_recv()
            for r in range(row_blocks):
                for group in range(cols):
                    span = x_all.shape[1]
                    x_t[r * blk:(r + 1) * blk, group * span:(group + 1) * span] = x_all[
                        group, :, r * blk:(r + 1) * blk
                    ].T

    pair_width = 2 * blk

    def weight_grads(n, carry):
        start = pl.multiple_of(n * pair_width, pair_width)
        g_cols = g_all[:, :, pl.ds(start, pair_width)].reshape(rows * tokens, pair_width)
        total = jnp.dot(x_t[...], g_cols, preferred_element_type=F32).astype(BF16)
        for r in range(row_blocks):
            for c in range(2):
                gw_ref[r * col_blocks + 2 * n + c] = total[
                    r * blk:(r + 1) * blk, c * blk:(c + 1) * blk
                ]
        return carry

    pairs = col_blocks // 2
    lax.fori_loop(0, pairs // 2, weight_grads, 0)
    for dh, dl in pending:
        finish(dh, dl)
    lax.fori_loop(pairs // 2, pairs, weight_grads, 0)

    for sub in range(per_group):
        total = part[col * per_group + sub]
        for dist in range(1, y_n):
            other = peer_y(dist)
            pltpu.make_async_remote_copy(
                src_ref=part.at[own], dst_ref=y_in.at[other, sub],
                send_sem=y_send.at[own], recv_sem=y_recv.at[other, sub],
                device_id=sibling, device_id_type=MESH,
            ).wait_recv()
            total = total + y_in[other, sub]
        gi_ref[sub * tokens:(sub + 1) * tokens, :] = total.astype(BF16)

    for t, step in enumerate([[(0, 0)]] + steps):
        for dh, dl in step:
            for chunk in range(CHUNKS):
                drain(dh, dl, chunk)
    for dist in range(1, y_n):
        x_to_y(dist).wait_send()
    for dist in range(y_n):
        x_to_sibling(dist).wait_send()

    def leave(block, carry):
        when(negate(mine(block)), lambda: pair_copy(block).wait_send())
        when(
            jnp.logical_and(mine(block), group_of(block) != col),
            lambda: y_copy(block).wait_send(),
        )
        return carry

    lax.fori_loop(0, rows, leave, 0)


def pick(coord_ref, gi_ref, blocks_ref, gi_out, gw_out):
    gi_out[...] = gi_ref[...]
    for s in range(gw_out.shape[0]):
        q = coord_ref[0, s]
        block = blocks_ref[jnp.maximum(q, 0)]
        gw_out[s] = jnp.where(q >= 0, block, jnp.zeros_like(block))


def solution(mesh):
    rows, cols = mesh.shape["row"], mesh.shape["col"]

    def local(x_act, grad_pre, weight_blocks, block_coord):
        blk = weight_blocks.shape[-1]
        slots = weight_blocks.shape[2]
        tokens, hidden = grad_pre.shape
        group, width = x_act.shape
        dma = pltpu.SemaphoreType.DMA
        y_n = cols // CORES
        anywhere = pl.BlockSpec(memory_space=pl.ANY)
        in_vmem = pl.BlockSpec(memory_space=pltpu.VMEM)
        grad_input, all_blocks = pl.pallas_call(
            functools.partial(kernel, rows, cols),
            out_shape=(
                jax.ShapeDtypeStruct((group, width), BF16),
                jax.ShapeDtypeStruct((width // blk * (hidden // blk), blk, blk), BF16),
            ),
            in_specs=[pl.BlockSpec(memory_space=pltpu.SMEM), anywhere, anywhere, anywhere],
            out_specs=(in_vmem, in_vmem),
            scratch_shapes=[
                pltpu.VMEM((rows, tokens, hidden), BF16),
                pltpu.VMEM((cols, group, width), BF16),
                pltpu.VMEM((width, cols * group), BF16),
                pltpu.VMEM((slots, blk, blk), BF16),
                pltpu.VMEM((slots, blk, blk), BF16),
                pltpu.VMEM((hidden, width), BF16),
                pltpu.VMEM((rows, tokens, width), F32),
                pltpu.VMEM((rows, tokens, width), F32),
                pltpu.VMEM((y_n, rows // cols, tokens, width), F32),
                dma((3,)),
                dma((4, rows, CHUNKS)),
                dma((rows, CHUNKS)),
                dma((2 * y_n,)),
                dma((cols,)),
                dma((rows,)),
                dma((rows,)),
                dma((rows,)),
                dma((y_n, rows // cols)),
            ],
            compiler_params=pltpu.CompilerParams(collective_id=0, has_side_effects=True),
        )(block_coord[0], x_act, grad_pre, weight_blocks.reshape(slots, blk, blk))
        grad_input, grad_weight = pl.pallas_call(
            pick,
            out_shape=(
                jax.ShapeDtypeStruct((group, width), BF16),
                jax.ShapeDtypeStruct((slots, blk, blk), BF16),
            ),
            in_specs=[pl.BlockSpec(memory_space=pltpu.SMEM), in_vmem, in_vmem],
            out_specs=(in_vmem, in_vmem),
        )(block_coord[0], grad_input, all_blocks)
        return grad_input, grad_weight.reshape(1, 1, slots, blk, blk)

    return jax.shard_map(
        local,
        mesh=mesh,
        in_specs=(
            P("col", "row"),
            P("row", "col"),
            P("row", "col", None, None, None),
            P("row", "col", None),
        ),
        out_specs=(P("col", "row"), P("row", "col", None, None, None)),
        check_vma=False,
    )
```

```python
import functools

import jax
import jax.numpy as jnp
from jax import lax
from jax.experimental import pallas as pl
from jax.experimental.pallas import tpu as pltpu
from jax.sharding import PartitionSpec as P

MESH = pl.DeviceIdType.MESH
CORES = 2
CHUNKS = 2
F32 = jnp.float32
BF16 = jnp.bfloat16


def either(a, b):
    if a is True or b is True:
        return True
    if a is False:
        return b
    if b is False:
        return a
    return jnp.logical_or(a, b)


def both(a, b):
    if a is False or b is False:
        return False
    if a is True:
        return b
    if b is True:
        return a
    return jnp.logical_and(a, b)


def negate(a):
    return (not a) if isinstance(a, bool) else jnp.logical_not(a)


def when(cond, body):
    if cond is True:
        body()
    elif cond is not False:
        pl.when(cond)(body)


def kernel(
    rows, cols, coord_ref, x_ref, g_ref, w_ref, gi_ref, gw_out,
    g_all, x_all, x_t, w_own, w_t, dense, part, pair_in, y_in, gw_ref,
    local_sem, g_send, g_recv, x_send, x_recv, pair_send, pair_recv, y_send, y_recv,
):
    hi_n = 4 if rows % 4 == 0 else 1
    lo_n = rows // hi_n
    y_n = cols // CORES
    slots, blk = w_own.shape[0], w_own.shape[1]
    tokens = g_all.shape[1]
    step_rows = tokens // CHUNKS
    row_blocks = x_t.shape[0] // blk
    col_blocks = g_all.shape[2] // blk
    per_group = rows // cols

    row = lax.axis_index("row")
    col = lax.axis_index("col")
    hi, lo = lax.div(row, lo_n), lax.rem(row, lo_n)
    y, core = lax.div(col, CORES), lax.rem(col, CORES)
    sibling = (row, y * CORES + (1 - core))
    own = row

    def peer_y(dist):
        return lax.rem(y + dist, y_n)

    directions = (
        (hi < hi_n - 1, (row + lo_n, col)),
        (hi > 0, (row - lo_n, col)),
        (lo < lo_n - 1, (row + 1, col)),
        (lo > 0, (row - 1, col)),
    )

    own_g = pltpu.make_async_copy(g_ref, g_all.at[own], local_sem.at[0])
    own_x = pltpu.make_async_copy(x_ref, x_all.at[col], local_sem.at[1])
    own_w = pltpu.make_async_copy(w_ref, w_own, local_sem.at[2])
    own_w.start()
    own_g.start()
    own_x.start()

    barrier = pltpu.get_barrier_semaphore()
    count = jnp.int32(y_n)
    for there, device in directions:
        count = count + there.astype(jnp.int32)

        def greet(device=device):
            pl.semaphore_signal(barrier, inc=1, device_id=device, device_id_type=MESH)

        when(there, greet)
    pl.semaphore_signal(barrier, inc=1, device_id=sibling, device_id_type=MESH)
    for dist in range(1, y_n):
        pl.semaphore_signal(
            barrier, inc=1, device_id=(row, peer_y(dist) * CORES + core), device_id_type=MESH
        )
    pl.semaphore_wait(barrier, count)

    def g_copy(block, chunk, direction, from_input=False):
        span = pl.ds(chunk * step_rows, step_rows)
        there = g_all.at[block, span]
        return pltpu.make_async_remote_copy(
            src_ref=g_ref.at[span] if from_input else there,
            dst_ref=there,
            send_sem=g_send.at[direction, block, chunk],
            recv_sem=g_recv.at[block, chunk],
            device_id=directions[direction][1],
            device_id_type=MESH,
        )

    def sends(dh, dl, chunk):
        origin = hi + dh
        swapped = False
        if chunk == CHUNKS - 1:
            swapped = jnp.logical_or(origin == 0, origin == hi_n - 1)
        along_hi = either(swapped, dl == 0)
        along_lo = either(negate(swapped), dh == 0)
        conds = (
            both(along_hi, dh <= 0), both(along_hi, dh >= 0),
            both(along_lo, dl <= 0), both(along_lo, dl >= 0),
        )
        return [both(cond, directions[n][0]) for n, cond in enumerate(conds)]

    def valid(dh, dl):
        cond = True
        if dh > 0:
            cond = both(cond, hi + dh < hi_n)
        if dh < 0:
            cond = both(cond, hi + dh >= 0)
        if dl > 0:
            cond = both(cond, lo + dl < lo_n)
        if dl < 0:
            cond = both(cond, lo + dl >= 0)
        return cond

    def block_of(dh, dl):
        return row + (dh * lo_n + dl)

    def forward(dh, dl, chunk):
        for n, cond in enumerate(sends(dh, dl, chunk)):
            when(cond, lambda n=n: g_copy(block_of(dh, dl), chunk, n, dh == 0 and dl == 0).start())

    def arrive(dh, dl, chunk):
        def body():
            g_copy(block_of(dh, dl), chunk, 0).wait_recv()
            forward(dh, dl, chunk)

        when(valid(dh, dl), body)

    def drain(dh, dl, chunk):
        def body():
            for n, cond in enumerate(sends(dh, dl, chunk)):
                when(cond, lambda n=n: g_copy(block_of(dh, dl), chunk, n, dh == 0 and dl == 0).wait_send())

        when(valid(dh, dl), body)

    def x_copy(index, group, device, from_input=False):
        return pltpu.make_async_remote_copy(
            src_ref=x_ref if from_input else x_all.at[group],
            dst_ref=x_all.at[group],
            send_sem=x_send.at[index],
            recv_sem=x_recv.at[group],
            device_id=device,
            device_id_type=MESH,
        )

    def x_to_y(dist):
        return x_copy(dist, col, (row, peer_y(dist) * CORES + core), True)

    def x_to_sibling(dist):
        return x_copy(y_n + dist, peer_y(dist) * CORES + core, sibling, dist == 0)

    def x_from_sibling(dist):
        return x_copy(0, peer_y(dist) * CORES + (1 - core), sibling)

    def group_of(block):
        return lax.div(block, per_group)

    def mine(block):
        return lax.rem(group_of(block), CORES) == core

    def pair_copy(block):
        return pltpu.make_async_remote_copy(
            src_ref=part.at[block],
            dst_ref=pair_in.at[block],
            send_sem=pair_send.at[block],
            recv_sem=pair_recv.at[block],
            device_id=sibling,
            device_id_type=MESH,
        )

    def y_copy(block):
        sub = lax.rem(block, per_group)
        return pltpu.make_async_remote_copy(
            src_ref=part.at[block],
            dst_ref=y_in.at[y, sub],
            send_sem=y_send.at[block],
            recv_sem=y_recv.at[y, sub],
            device_id=(row, group_of(block)),
            device_id_type=MESH,
        )

    def compute(dh, dl):
        def body():
            block = block_of(dh, dl)
            part[block] = jnp.dot(g_all[block], dense[...], preferred_element_type=F32)
            when(negate(mine(block)), lambda: pair_copy(block).start())

        when(valid(dh, dl), body)

    def finish(dh, dl):
        def body():
            block = block_of(dh, dl)

            def reduce():
                pair_copy(block).wait_recv()
                part[block] = part[block] + pair_in[block]
                when(group_of(block) != col, lambda: y_copy(block).start())

            when(mine(block), reduce)

        when(valid(dh, dl), body)

    for chunk in range(CHUNKS):
        forward(0, 0, chunk)
    for dist in range(1, y_n):
        x_to_y(dist).start()
    x_to_sibling(0).start()

    own_w.wait()

    def turn(s, carry):
        w_t[s] = w_own[s].T
        return carry

    lax.fori_loop(0, slots, turn, 0)

    def spread(c, carry):
        for r in range(row_blocks):
            total = jnp.zeros((blk, blk), BF16)
            for s in range(slots):
                hit = (coord_ref[0, s] == r * col_blocks + c).astype(F32)
                total = total + w_t[s] * jnp.full((blk, blk), hit, F32).astype(BF16)
            dense[pl.ds(pl.multiple_of(c * blk, blk), blk), r * blk:(r + 1) * blk] = total
        return carry

    steps = []
    for t in range(1, hi_n + lo_n - 1):
        step = []
        for far in range(min(t, hi_n - 1), -1, -1):
            side = t - far
            if side >= lo_n:
                continue
            for dh in sorted({far, -far}):
                for dl in sorted({side, -side}):
                    step.append((dh, dl))
        steps.append(step)

    def x_turn():
        span = x_all.shape[1]
        for dist in range(y_n):
            x_from_sibling(dist).wait_recv()
        for r in range(row_blocks):
            for group in range(cols):
                x_t[r * blk:(r + 1) * blk, group * span:(group + 1) * span] = x_all[
                    group, :, r * blk:(r + 1) * blk
                ].T

    def arrivals(step, chunk):
        for dh, dl in step:
            arrive(dh, dl, chunk)

    def computes(blocks):
        for dh, dl in blocks:
            compute(dh, dl)

    def finishes(blocks):
        for dh, dl in blocks:
            finish(dh, dl)

    lax.fori_loop(0, col_blocks // 2, spread, 0)
    computed, waiting = [], [(0, 0)]
    last = len(steps) - 1
    for index, step in enumerate(steps):
        if index == last:
            computes(waiting)
            finishes(computed + waiting)
            computed, waiting = [], []
        cut = len(waiting) // 2
        for chunk in range(CHUNKS):
            arrivals(step, chunk)
            if chunk == 0:
                if index == 0:
                    lax.fori_loop(col_blocks // 2, col_blocks, spread, 0)
                    own_g.wait()
                    own_x.wait()
                computes(waiting[:cut])
        computes(waiting[cut:])
        finishes(computed)
        computed, waiting = waiting, step
        if index == 0:
            for dist in range(1, y_n):
                x_copy(0, peer_y(dist) * CORES + core, sibling).wait_recv()
                x_to_sibling(dist).start()
        if index == min(1, last):
            x_turn()
    computes(waiting)

    pair_width = 2 * blk

    def weight_grads(n, carry):
        start = pl.multiple_of(n * pair_width, pair_width)
        g_cols = g_all[:, :, pl.ds(start, pair_width)].reshape(rows * tokens, pair_width)
        total = jnp.dot(x_t[...], g_cols, preferred_element_type=F32).astype(BF16)
        for r in range(row_blocks):
            for c in range(2):
                gw_ref[r * col_blocks + 2 * n + c] = total[
                    r * blk:(r + 1) * blk, c * blk:(c + 1) * blk
                ]
        return carry

    pairs = col_blocks // 2
    early = pairs // 4
    lax.fori_loop(0, early, weight_grads, 0)
    finishes(computed + waiting)
    lax.fori_loop(early, pairs, weight_grads, 0)
    gw_copy = pltpu.make_async_copy(gw_ref, gw_out, local_sem.at[3])
    gw_copy.start()

    for sub in range(per_group):
        total = part[col * per_group + sub]
        for dist in range(1, y_n):
            other = peer_y(dist)
            pltpu.make_async_remote_copy(
                src_ref=part.at[own], dst_ref=y_in.at[other, sub],
                send_sem=y_send.at[own], recv_sem=y_recv.at[other, sub],
                device_id=sibling, device_id_type=MESH,
            ).wait_recv()
            total = total + y_in[other, sub]
        gi_ref[sub * tokens:(sub + 1) * tokens, :] = total.astype(BF16)

    for t, step in enumerate([[(0, 0)]] + steps):
        for dh, dl in step:
            for chunk in range(CHUNKS):
                drain(dh, dl, chunk)
    for dist in range(1, y_n):
        x_to_y(dist).wait_send()
    for dist in range(y_n):
        x_to_sibling(dist).wait_send()

    def leave(block, carry):
        when(negate(mine(block)), lambda: pair_copy(block).wait_send())
        when(
            jnp.logical_and(mine(block), group_of(block) != col),
            lambda: y_copy(block).wait_send(),
        )
        return carry

    lax.fori_loop(0, rows, leave, 0)
    gw_copy.wait()


def pick(coord_ref, gi_ref, blocks_ref, gi_out, gw_out, held, into, out):
    slots = held.shape[0]

    def load(s):
        return pltpu.make_async_copy(
            blocks_ref.at[jnp.maximum(coord_ref[0, s], 0)], held.at[s], into.at[s]
        )

    def store(s):
        return pltpu.make_async_copy(held.at[s], gw_out.at[s], out.at[s])

    for s in range(slots):
        load(s).start()
    gi_out[...] = gi_ref[...]
    for s in range(slots):
        load(s).wait()

        @pl.when(coord_ref[0, s] < 0)
        def _():
            held[s] = jnp.zeros(held.shape[1:], BF16)

        store(s).start()
    for s in range(slots):
        store(s).wait()


def solution(mesh):
    rows, cols = mesh.shape["row"], mesh.shape["col"]

    def local(x_act, grad_pre, weight_blocks, block_coord):
        blk = weight_blocks.shape[-1]
        slots = weight_blocks.shape[2]
        tokens, hidden = grad_pre.shape
        group, width = x_act.shape
        dma = pltpu.SemaphoreType.DMA
        y_n = cols // CORES
        anywhere = pl.BlockSpec(memory_space=pl.ANY)
        in_vmem = pl.BlockSpec(memory_space=pltpu.VMEM)
        grad_input, all_blocks = pl.pallas_call(
            functools.partial(kernel, rows, cols),
            out_shape=(
                jax.ShapeDtypeStruct((group, width), BF16),
                jax.ShapeDtypeStruct((width // blk * (hidden // blk), blk, blk), BF16),
            ),
            in_specs=[pl.BlockSpec(memory_space=pltpu.SMEM), anywhere, anywhere, anywhere],
            out_specs=(in_vmem, anywhere),
            scratch_shapes=[
                pltpu.VMEM((rows, tokens, hidden), BF16),
                pltpu.VMEM((cols, group, width), BF16),
                pltpu.VMEM((width, cols * group), BF16),
                pltpu.VMEM((slots, blk, blk), BF16),
                pltpu.VMEM((slots, blk, blk), BF16),
                pltpu.VMEM((hidden, width), BF16),
                pltpu.VMEM((rows, tokens, width), F32),
                pltpu.VMEM((rows, tokens, width), F32),
                pltpu.VMEM((y_n, rows // cols, tokens, width), F32),
                pltpu.VMEM((width // blk * (hidden // blk), blk, blk), BF16),
                dma((4,)),
                dma((4, rows, CHUNKS)),
                dma((rows, CHUNKS)),
                dma((2 * y_n,)),
                dma((cols,)),
                dma((rows,)),
                dma((rows,)),
                dma((rows,)),
                dma((y_n, rows // cols)),
            ],
            compiler_params=pltpu.CompilerParams(collective_id=0, has_side_effects=True),
        )(block_coord[0], x_act, grad_pre, weight_blocks.reshape(slots, blk, blk))
        grad_input, grad_weight = pl.pallas_call(
            pick,
            out_shape=(
                jax.ShapeDtypeStruct((group, width), BF16),
                jax.ShapeDtypeStruct((slots, blk, blk), BF16),
            ),
            in_specs=[pl.BlockSpec(memory_space=pltpu.SMEM), in_vmem, anywhere],
            out_specs=(in_vmem, anywhere),
            scratch_shapes=[pltpu.VMEM((slots, blk, blk), BF16), dma((slots,)), dma((slots,))],
        )(block_coord[0], grad_input, all_blocks)
        return grad_input, grad_weight.reshape(1, 1, slots, blk, blk)

    return jax.shard_map(
        local,
        mesh=mesh,
        in_specs=(
            P("col", "row"),
            P("row", "col"),
            P("row", "col", None, None, None),
            P("row", "col", None),
        ),
        out_specs=(P("col", "row"), P("row", "col", None, None, None)),
        check_vma=False,
    )
```
